32 devices in a mesh: freq: 4 (over x, core), rows: 8 (over z, y).
Axes of the slice: x: 2, y: 2, z: 4, core: 2. Of those that a mesh axis runs over, the one named last changes fastest.
Arguments:
- time_loads: float32 [256, 192, 2048], P('freq', None, 'rows'), may hold values from -6 to 6
- factor: float32 [16, 2, 2048, 2048], P('freq', None, 'rows'), may hold values from -0.09375 to 0.09375
- diag_inverse: float32 [16, 2, 2048, 256], P('freq', None, 'rows'), may hold values from -0.25 to 0.25
- pivot_order: int32 [8], replicated, may hold values from 0 to 7, each once
Outputs:
- solution: float32 [16, 2, 192, 2048], P('freq', None, None, 'rows')
The draws below stay inside these ranges and needn't reach their ends.
Inputs may be any that keep to these rules, and one draw needn't show every extreme that they name: `pivot_order`: a permutation of the 8 row blocks.
All inputs are finite; a program needn't handle non-finite values.
Results may differ from the reference program's by a relative error of at most 0.0001.
Values sent between devices are 32-bit elements; how exact they have to be, the bound alone decides.
A program may use at most 128 MiB of HBM per device.

```python
import jax
import jax.numpy as jnp
from jax import lax

BS = 256
FREQS = 16
STEPS = 256
CASES = 192
NB = 8
ROWS = 2048


def block_scale(stream_key, dims, shards, low, high):
    def one(position, shards_of):
        draws = jax.random.uniform(jax.random.fold_in(jax.random.fold_in(stream_key, 6), position), (shards_of,), jnp.float32, low / len(shards), high / len(shards))
        return jnp.repeat(jnp.exp(draws), dims[position] // shards_of).reshape((-1,) + (1,) * (len(dims) - position - 1))

    level = one(*shards[0])
    for cut in shards[1:]:
        level = level * one(*cut)
    return level


def gaussian(rng, extent, scale, reach, shards=(), held_as=jnp.bfloat16):
    gain = block_scale(rng, extent, shards, -0.22, 0.18) if shards else 1.0
    array = jax.random.normal(rng, extent, jnp.float32) * scale * gain
    return jnp.minimum(jnp.maximum(array, -reach), reach).astype(held_as)


def setup_inputs(seed: int = 0) -> dict:
    splits = jax.random.split(jax.random.key(seed), 5)
    return {
        "time_loads": gaussian(splits[0], (STEPS, CASES, ROWS), 1.0, 6.0, ((0, 4), (2, 8)), jnp.float32),
        "factor": gaussian(splits[1], (FREQS, 2, ROWS, ROWS), (2 * ROWS) ** -0.5, 0.09375, ((0, 4), (2, 8)), jnp.float32),
        "diag_inverse": gaussian(splits[2], (FREQS, 2, ROWS, BS), (2 * BS) ** -0.5, 0.25, ((0, 4), (2, 8)), jnp.float32),
        "pivot_order": jax.random.permutation(splits[3], NB).astype(jnp.int32),
    }


def tables(count, length):
    freq_range = jnp.arange(count, dtype=jnp.float32)
    step_range = jnp.arange(length, dtype=jnp.float32)
    angles = 2.0 * jnp.pi * ((freq_range[:, None] * step_range[None, :]) % length) / length
    damping = jnp.exp(step_range * (jnp.log(0.1) / length))
    return jnp.cos(angles) * damping[None, :], -jnp.sin(angles) * damping[None, :]


def product(matrix, vector):
    return jnp.einsum("fab,fcb->fca", matrix, vector, precision=lax.Precision.HIGHEST)


def complex_apply(matrix, vector):
    matrix_real, matrix_imag = matrix[:, 0], matrix[:, 1]
    vector_real, vector_imag = vector[:, 0], vector[:, 1]
    real_part = product(matrix_real, vector_real) - product(matrix_imag, vector_imag)
    imag_part = product(matrix_real, vector_imag) + product(matrix_imag, vector_real)
    return jnp.stack([real_part, imag_part], axis=1)


def reference(time_loads, factor, diag_inverse, pivot_order):
    cosine_table, sine_table = tables(FREQS, STEPS)
    spectra = jnp.stack([
        jnp.einsum("fn,ncr->fcr", cosine_table, time_loads, precision=lax.Precision.HIGHEST),
        jnp.einsum("fn,ncr->fcr", sine_table, time_loads, precision=lax.Precision.HIGHEST)], axis=1)
    residual = spectra
    solution = jnp.zeros_like(spectra)
    for turn in range(NB):
        first_row = (pivot_order[turn] * BS).astype(jnp.int32)
        current = lax.dynamic_slice_in_dim(residual, first_row, BS, 3)
        inverse_block = lax.dynamic_slice_in_dim(diag_inverse, first_row, BS, 2)
        solved = complex_apply(inverse_block, current)
        solution = lax.dynamic_update_slice_in_dim(solution, solved, first_row, 3)
        column = lax.dynamic_slice_in_dim(factor, first_row, BS, 3)
        residual = residual - complex_apply(column, solved)
    return solution
```

```python
import functools

import jax
import jax.numpy as jnp
from jax import lax
from jax.experimental import pallas as pl
from jax.experimental.pallas import tpu as pltpu
from jax.sharding import PartitionSpec as P

FREQS = 16
STEPS = 256
MESH = pl.DeviceIdType.MESH


def tables(count, length):
    freq_range = jnp.arange(count, dtype=jnp.float32)
    step_range = jnp.arange(length, dtype=jnp.float32)
    angles = 2.0 * jnp.pi * (freq_range[:, None] * step_range[None, :] % length) / length
    damping = jnp.exp(step_range * (jnp.log(0.1) / length))
    return (jnp.cos(angles) * damping[None, :], -jnp.sin(angles) * damping[None, :])


def zigzag(major, minor, extent):
    return minor + lax.rem(major, 2) * (extent - 1 - 2 * minor)


def chain_position(kind, index, outer, inner):
    z, y = lax.div(index, inner), lax.rem(index, inner)
    if kind == 1:
        y = inner - 1 - y
    if kind == 3:
        z = outer - 1 - z
    if kind < 2:
        return z * inner + zigzag(z, y, inner)
    return y * outer + zigzag(y, z, outer)


def chain_index(kind, position, outer, inner):
    if kind < 2:
        z = lax.div(position, inner)
        y = zigzag(z, lax.rem(position, inner), inner)
    else:
        y = lax.div(position, outer)
        z = zigzag(y, lax.rem(position, outer), outer)
    if kind == 1:
        y = inner - 1 - y
    if kind == 3:
        z = outer - 1 - z
    return z * inner + y


def substitute(dims, pivot_ref, high_ref, low_ref, start_ref, out_ref, right_buf, left_buf,
               send_sem, recv_sem):
    freqs, blocks, units, cases, outer, inner = dims
    width = out_ref.shape[3]
    me = lax.axis_index("rows")
    slots = right_buf.shape[1]
    pieces = blocks * units
    last = blocks - 1

    barrier = pltpu.get_barrier_semaphore()
    for shift in range(1, blocks):
        pl.semaphore_signal(
            barrier, inc=1, device_id={"rows": lax.rem(me + shift, blocks)}, device_id_type=MESH
        )
    out_ref[...] = start_ref[...]
    pl.semaphore_wait(barrier, last)

    my_turn = jnp.int32(0)
    for turn in range(blocks):
        my_turn = my_turn + jnp.where(pivot_ref[turn] == me, turn, 0)

    def copy(direction, f, piece, target):
        buf = (right_buf, left_buf)[direction]
        slot = lax.rem(piece, slots)
        return pltpu.make_async_remote_copy(
            src_ref=buf.at[f, slot],
            dst_ref=buf.at[f, slot],
            send_sem=send_sem.at[direction, f, lax.rem(piece, 2)],
            recv_sem=recv_sem.at[direction, f, slot],
            device_id={"rows": target},
            device_id_type=MESH,
        )

    chains = []
    for f in range(freqs):
        kind = f % 4
        position = chain_position(kind, me, outer, inner)
        right = chain_index(kind, lax.rem(position + 1, blocks), outer, inner)
        left = chain_index(kind, lax.rem(position + last, blocks), outer, inner)
        chains.append((kind, position, right, left))

    def rows_of(piece):
        return pl.ds(pl.multiple_of(lax.rem(piece, units) * cases, 8), cases)

    def flow(direction, f, piece, target, is_first, is_last):
        buf = (right_buf, left_buf)[direction]
        slot = lax.rem(piece, slots)

        @pl.when((piece >= 0) & (piece < pieces))
        def _():
            @pl.when(jnp.logical_not(is_first))
            def _():
                copy(direction, f, piece, target).wait_recv()
                mine = pivot_ref[lax.div(piece, units)] == me
                buf[f, slot] = jnp.where(mine, out_ref[f, :, rows_of(piece), :], buf[f, slot])

            @pl.when(is_first)
            def _():
                buf[f, slot] = out_ref[f, :, rows_of(piece), :]

            @pl.when(jnp.logical_not(is_last))
            def _():
                @pl.when(piece >= 2)
                def _():
                    copy(direction, f, piece - 2, target).wait_send()

                copy(direction, f, piece, target).start()

    def finish(f, kind, position, piece):
        @pl.when((piece >= 0) & (piece < pieces))
        def _():
            turn = lax.div(piece, units)
            slot = lax.rem(piece, slots)
            owner = chain_position(kind, pivot_ref[turn], outer, inner)
            solved = jnp.where(owner <= position, right_buf[f, slot], left_buf[f, slot])
            solved = solved.reshape(2 * cases, width)
            high = solved.astype(jnp.bfloat16)
            low = (solved - high.astype(jnp.float32)).astype(jnp.bfloat16)
            both = jnp.dot(
                jnp.concatenate([high, low], axis=0), high_ref[turn, f],
                preferred_element_type=jnp.float32,
            )
            rest = jnp.dot(high, low_ref[turn, f], preferred_element_type=jnp.float32)
            total = both[: 2 * cases] + both[2 * cases :] + rest
            from_real, from_imag = total[:cases], total[cases:]
            real = from_real[:, :width] - from_imag[:, width:]
            imag = from_real[:, width:] + from_imag[:, :width]
            rows = rows_of(piece)
            open_still = turn < my_turn
            real_now, imag_now = out_ref[f, 0, rows, :], out_ref[f, 1, rows, :]
            out_ref[f, 0, rows, :] = jnp.where(open_still, real_now - real, real_now)
            out_ref[f, 1, rows, :] = jnp.where(open_still, imag_now - imag, imag_now)

    def tick(t, carry):
        for f, (kind, position, right, left) in enumerate(chains):
            at_start, at_end = position == 0, position == last
            flow(0, f, t - position, right, at_start, at_end)
            flow(1, f, t - (last - position), left, at_end, at_start)
            finish(f, kind, position, t - jnp.maximum(position, last - position))
        return carry

    lax.fori_loop(0, pieces + last, tick, 0)

    for f, (kind, position, right, left) in enumerate(chains):
        for piece in (pieces - 2, pieces - 1):
            @pl.when(position < last)
            def _():
                copy(0, f, jnp.int32(piece), right).wait_send()

            @pl.when(position > 0)
            def _():
                copy(1, f, jnp.int32(piece), left).wait_send()


def body(time_loads, factor, diag_inverse, pivot_order):
    high = lax.Precision.HIGH
    local_freqs = factor.shape[0]
    local_steps = time_loads.shape[0]
    all_cases = time_loads.shape[1]
    blocks = lax.axis_size("rows")
    width = diag_inverse.shape[3]
    cosine_table, sine_table = tables(FREQS, STEPS)
    table = jnp.stack([cosine_table, sine_table], axis=1)
    offset = lax.axis_index("freq") * local_steps
    part = lax.dynamic_slice_in_dim(table, offset, local_steps, 2)
    part = part.reshape(-1, local_steps)
    spectra = jnp.einsum("gn,ncr->gcr", part, time_loads, precision=high)
    spectra = spectra.reshape(FREQS, 2, all_cases, width)
    spectra = lax.psum_scatter(spectra, "freq", scatter_dimension=0, tiled=True)

    columns = factor.reshape(local_freqs, 2, width, blocks, width)
    columns = jnp.take(columns, pivot_order, axis=3)
    inverse_real, inverse_imag = diag_inverse[:, 0], diag_inverse[:, 1]

    def fold(matrix, part_of):
        return jnp.einsum("fab,fbkc->kfca", matrix, columns[:, part_of], precision=high)

    real = fold(inverse_real, 0) - fold(inverse_imag, 1)
    imag = fold(inverse_real, 1) + fold(inverse_imag, 0)
    scaled = jnp.concatenate([real, imag], axis=3)
    rounded = lax.reduce_precision(scaled, 8, 7)
    scaled_high = rounded.astype(jnp.bfloat16)
    scaled_low = (scaled - rounded).astype(jnp.bfloat16)

    def apply(matrix, part_of):
        return jnp.einsum("fab,fcb->fca", matrix, spectra[:, part_of], precision=high)

    start = jnp.stack(
        [
            apply(inverse_real, 0) - apply(inverse_imag, 1),
            apply(inverse_real, 1) + apply(inverse_imag, 0),
        ],
        axis=1,
    )

    units = blocks
    cases = -(-all_cases // (8 * units)) * 8
    padded = cases * units
    if padded > all_cases:
        start = jnp.pad(start, ((0, 0), (0, 0), (0, padded - all_cases), (0, 0)))
    inner = 1
    while 4 * inner * inner <= blocks:
        inner *= 2
    slots = 2 * units
    dims = (local_freqs, blocks, units, cases, blocks // inner, inner)
    vmem = pl.BlockSpec(memory_space=pltpu.VMEM)
    solution = pl.pallas_call(
        functools.partial(substitute, dims),
        out_shape=jax.ShapeDtypeStruct(start.shape, jnp.float32),
        in_specs=[pl.BlockSpec(memory_space=pltpu.SMEM), vmem, vmem, vmem],
        out_specs=vmem,
        scratch_shapes=[
            pltpu.VMEM((local_freqs, slots, 2, cases, width), jnp.float32),
            pltpu.VMEM((local_freqs, slots, 2, cases, width), jnp.float32),
            pltpu.SemaphoreType.DMA((2, local_freqs, 2)),
            pltpu.SemaphoreType.DMA((2, local_freqs, slots)),
        ],
        compiler_params=pltpu.CompilerParams(
            collective_id=0, has_side_effects=True, vmem_limit_bytes=60 * 1024 * 1024
        ),
    )(pivot_order, scaled_high, scaled_low, start)
    return solution[:, :, :all_cases]


def solution(mesh):
    placed = (
        P("freq", None, "rows"),
        P("freq", None, "rows", None),
        P("freq", None, "rows", None),
        P(),
    )
    return jax.shard_map(
        body, mesh=mesh, in_specs=placed, out_specs=P("freq", None, None, "rows"), check_vma=False
    )
```

```python
import functools

import jax
import jax.numpy as jnp
from jax import lax
from jax.experimental import pallas as pl
from jax.experimental.pallas import tpu as pltpu
from jax.sharding import PartitionSpec as P

FREQS = 16
STEPS = 256
MESH = pl.DeviceIdType.MESH


def tables(count, length):
    freq_range = jnp.arange(count, dtype=jnp.float32)
    step_range = jnp.arange(length, dtype=jnp.float32)
    angles = 2.0 * jnp.pi * (freq_range[:, None] * step_range[None, :] % length) / length
    damping = jnp.exp(step_range * (jnp.log(0.1) / length))
    return (jnp.cos(angles) * damping[None, :], -jnp.sin(angles) * damping[None, :])


def zigzag(major, minor, extent):
    return minor + lax.rem(major, 2) * (extent - 1 - 2 * minor)


def chain_position(kind, index, outer, inner):
    z, y = lax.div(index, inner), lax.rem(index, inner)
    if kind == 1:
        y = inner - 1 - y
    if kind == 3:
        z = outer - 1 - z
    if kind < 2:
        return z * inner + zigzag(z, y, inner)
    return y * outer + zigzag(y, z, outer)


def chain_index(kind, position, outer, inner):
    if kind < 2:
        z = lax.div(position, inner)
        y = zigzag(z, lax.rem(position, inner), inner)
    else:
        y = lax.div(position, outer)
        z = zigzag(y, lax.rem(position, outer), outer)
    if kind == 1:
        y = inner - 1 - y
    if kind == 3:
        z = outer - 1 - z
    return z * inner + y


def split(value):
    high = value.astype(jnp.bfloat16)
    return high, (value - high.astype(jnp.float32)).astype(jnp.bfloat16)


def triple(value, right_high, right_low):
    high, low = split(value)
    count = value.shape[0]
    both = jnp.dot(
        jnp.concatenate([high, low], axis=0), right_high, preferred_element_type=jnp.float32
    )
    rest = jnp.dot(high, right_low, preferred_element_type=jnp.float32)
    return both[:count] + both[count:] + rest


def substitute(dims, pivot_ref, high_ref, low_ref, start_ref, out_ref, right_buf, left_buf,
               send_sem, recv_sem):
    freqs, blocks, units, cases, outer, inner = dims
    width = out_ref.shape[3]
    me = lax.axis_index("rows")
    slots = right_buf.shape[1]
    pieces = blocks * units
    last = blocks - 1

    barrier = pltpu.get_barrier_semaphore()
    for shift in range(1, blocks):
        pl.semaphore_signal(
            barrier, inc=1, device_id={"rows": lax.rem(me + shift, blocks)}, device_id_type=MESH
        )
    out_ref[...] = start_ref[...]
    pl.semaphore_wait(barrier, last)

    my_turn = jnp.int32(0)
    for turn in range(blocks):
        my_turn = my_turn + jnp.where(pivot_ref[turn] == me, turn, 0)

    def copy(direction, f, piece, target):
        buf = (right_buf, left_buf)[direction]
        slot = lax.rem(piece, slots)
        return pltpu.make_async_remote_copy(
            src_ref=buf.at[f, slot],
            dst_ref=buf.at[f, slot],
            send_sem=send_sem.at[direction, f, lax.rem(piece, 2)],
            recv_sem=recv_sem.at[direction, f, slot],
            device_id={"rows": target},
            device_id_type=MESH,
        )

    chains = []
    for f in range(freqs):
        kind = f % 4
        position = chain_position(kind, me, outer, inner)
        right = chain_index(kind, lax.rem(position + 1, blocks), outer, inner)
        left = chain_index(kind, lax.rem(position + last, blocks), outer, inner)
        chains.append((kind, position, right, left))

    def rows_of(piece):
        return pl.ds(pl.multiple_of(lax.rem(piece, units) * cases, 8), cases)

    def flow(direction, f, piece, target, is_first, is_last):
        buf = (right_buf, left_buf)[direction]
        slot = lax.rem(piece, slots)

        @pl.when((piece >= 0) & (piece < pieces))
        def _():
            @pl.when(jnp.logical_not(is_first))
            def _():
                copy(direction, f, piece, target).wait_recv()
                mine = pivot_ref[lax.div(piece, units)] == me
                buf[f, slot] = jnp.where(mine, out_ref[f, :, rows_of(piece), :], buf[f, slot])

            @pl.when(is_first)
            def _():
                buf[f, slot] = out_ref[f, :, rows_of(piece), :]

            @pl.when(jnp.logical_not(is_last))
            def _():
                @pl.when(piece >= 2)
                def _():
                    copy(direction, f, piece - 2, target).wait_send()

                copy(direction, f, piece, target).start()

    def finish(f, kind, position, piece):
        @pl.when((piece >= 0) & (piece < pieces))
        def _():
            turn = lax.div(piece, units)
            slot = lax.rem(piece, slots)
            owner = chain_position(kind, pivot_ref[turn], outer, inner)
            solved = jnp.where(owner <= position, right_buf[f, slot], left_buf[f, slot])
            turn_block = pivot_ref[turn]
            total = triple(
                solved.reshape(2 * cases, width), high_ref[turn_block, f], low_ref[turn_block, f]
            )
            from_real, from_imag = total[:cases], total[cases:]
            real = from_real[:, :width] - from_imag[:, width:]
            imag = from_real[:, width:] + from_imag[:, :width]
            rows = rows_of(piece)
            open_still = turn < my_turn
            real_now, imag_now = out_ref[f, 0, rows, :], out_ref[f, 1, rows, :]
            out_ref[f, 0, rows, :] = jnp.where(open_still, real_now - real, real_now)
            out_ref[f, 1, rows, :] = jnp.where(open_still, imag_now - imag, imag_now)

    def tick(t, carry):
        for f, (kind, position, right, left) in enumerate(chains):
            at_start, at_end = position == 0, position == last
            flow(0, f, t - position, right, at_start, at_end)
            flow(1, f, t - (last - position), left, at_end, at_start)
            finish(f, kind, position, t - jnp.maximum(position, last - position))
        return carry

    lax.fori_loop(0, pieces + last, tick, 0)

    for f, (kind, position, right, left) in enumerate(chains):
        for piece in (pieces - 2, pieces - 1):
            @pl.when(position < last)
            def _():
                copy(0, f, jnp.int32(piece), right).wait_send()

            @pl.when(position > 0)
            def _():
                copy(1, f, jnp.int32(piece), left).wait_send()


def exchange(dims, spectra_ref, inverse_high, inverse_low, factor_ref, high_ref, low_ref,
             start_ref, core_buf, chip_buf, core_send, core_recv, chip_send, chip_recv):
    freqs, blocks, chips = dims
    cases, width = start_ref.shape[2], start_ref.shape[3]
    me = lax.axis_index("freq")
    chip, core = lax.div(me, 2), lax.rem(me, 2)
    step = pl.program_id(0) * blocks + pl.program_id(1)
    steps = freqs * blocks

    def core_copy(to_chip, f):
        return pltpu.make_async_remote_copy(
            src_ref=spectra_ref.at[to_chip * 2 + 1 - core, f],
            dst_ref=core_buf.at[to_chip, f],
            send_sem=core_send.at[to_chip, f],
            recv_sem=core_recv.at[to_chip, f],
            device_id={"freq": chip * 2 + 1 - core},
            device_id_type=MESH,
        )

    def chip_copy(shift, f):
        to_chip = lax.rem(chip + shift, chips)
        slot = chips - 1 - shift
        return pltpu.make_async_remote_copy(
            src_ref=core_buf.at[to_chip, f],
            dst_ref=chip_buf.at[slot, f],
            send_sem=chip_send.at[slot, f],
            recv_sem=chip_recv.at[slot, f],
            device_id={"freq": to_chip * 2 + core},
            device_id_type=MESH,
        )

    @pl.when(step == 0)
    def _():
        barrier = pltpu.get_barrier_semaphore()
        pl.semaphore_signal(
            barrier, inc=1, device_id={"freq": chip * 2 + 1 - core}, device_id_type=MESH
        )
        for shift in range(1, chips):
            pl.semaphore_signal(
                barrier, inc=1, device_id={"freq": lax.rem(chip + shift, chips) * 2 + core},
                device_id_type=MESH,
            )
        pl.semaphore_wait(barrier, chips)
        for f in range(freqs):
            for shift in range(1, chips + 1):
                core_copy(lax.rem(chip + shift, chips), f).start()

    for f in range(freqs):
        @pl.when(step == 1 + f)
        def _():
            for shift in range(1, chips):
                to_chip = lax.rem(chip + shift, chips)
                core_copy(to_chip, f).wait_recv()
                core_buf[to_chip, f] = core_buf[to_chip, f] + spectra_ref[to_chip * 2 + core, f]
                chip_copy(shift, f).start()

    taken = factor_ref[0]
    turned = jnp.concatenate([taken[0].T, taken[1].T], axis=0)
    f_now = pl.program_id(0)
    total = triple(turned, inverse_high[f_now], inverse_low[f_now])
    from_real, from_imag = total[:width], total[width:]
    real = from_real[:, :width] - from_imag[:, width:]
    imag = from_real[:, width:] + from_imag[:, :width]
    high_ref[0, 0], low_ref[0, 0] = split(jnp.concatenate([real, imag], axis=1))

    for f in range(freqs):
        @pl.when(step == steps - freqs + f)
        def _():
            core_copy(chip, f).wait_recv()
            value = spectra_ref[me, f] + core_buf[chip, f]
            for shift in range(1, chips):
                chip_copy(shift, f).wait_recv()
                value = value + chip_buf[chips - 1 - shift, f]
            solved = triple(value.reshape(2 * cases, width), inverse_high[f], inverse_low[f])
            start_ref[f, 0] = solved[:cases, :width] - solved[cases:, width:]
            start_ref[f, 1] = solved[:cases, width:] + solved[cases:, :width]
            for to_chip in range(chips):
                core_copy(to_chip, f).wait_send()
            for shift in range(1, chips):
                chip_copy(shift, f).wait_send()


def body(time_loads, factor, diag_inverse, pivot_order):
    high = lax.Precision.HIGH
    local_freqs = factor.shape[0]
    local_steps = time_loads.shape[0]
    all_cases = time_loads.shape[1]
    blocks = lax.axis_size("rows")
    owners = lax.axis_size("freq")
    width = diag_inverse.shape[3]
    cosine_table, sine_table = tables(FREQS, STEPS)
    table = jnp.stack([cosine_table, sine_table], axis=1)
    offset = lax.axis_index("freq") * local_steps
    part = lax.dynamic_slice_in_dim(table, offset, local_steps, 2)
    part = part.reshape(-1, local_steps)
    spectra = jnp.einsum("gn,ncr->gcr", part, time_loads, precision=high)
    spectra = spectra.reshape(owners, local_freqs, 2, all_cases, width)

    inverse = jnp.concatenate(
        [diag_inverse[:, 0].swapaxes(1, 2), diag_inverse[:, 1].swapaxes(1, 2)], axis=2
    )
    rounded = lax.reduce_precision(inverse, 8, 7)
    inverse_high = rounded.astype(jnp.bfloat16)
    inverse_low = (inverse - rounded).astype(jnp.bfloat16)

    chips = owners // 2
    vmem = pl.BlockSpec(memory_space=pltpu.VMEM)
    block = pl.BlockSpec((1, 1, width, 2 * width), lambda f, k: (k, f, 0, 0))
    scaled = jax.ShapeDtypeStruct((blocks, local_freqs, width, 2 * width), jnp.bfloat16)
    scaled_high, scaled_low, start = pl.pallas_call(
        functools.partial(exchange, (local_freqs, blocks, chips)),
        grid=(local_freqs, blocks),
        out_shape=(
            scaled, scaled,
            jax.ShapeDtypeStruct((local_freqs, 2, all_cases, width), jnp.float32),
        ),
        in_specs=[
            vmem, vmem, vmem,
            pl.BlockSpec((1, 2, width, width), lambda f, k: (f, 0, 0, k)),
        ],
        out_specs=(block, block, vmem),
        scratch_shapes=[
            pltpu.VMEM((chips, local_freqs, 2, all_cases, width), jnp.float32),
            pltpu.VMEM((max(chips - 1, 1), local_freqs, 2, all_cases, width), jnp.float32),
            pltpu.SemaphoreType.DMA((chips, local_freqs)),
            pltpu.SemaphoreType.DMA((chips, local_freqs)),
            pltpu.SemaphoreType.DMA((max(chips - 1, 1), local_freqs)),
            pltpu.SemaphoreType.DMA((max(chips - 1, 1), local_freqs)),
        ],
        compiler_params=pltpu.CompilerParams(
            collective_id=1, has_side_effects=True, vmem_limit_bytes=60 * 1024 * 1024,
            dimension_semantics=("arbitrary", "arbitrary"),
        ),
    )(spectra, inverse_high, inverse_low, factor)

    units = blocks
    cases = -(-all_cases // (8 * units)) * 8
    padded = cases * units
    if padded > all_cases:
        start = jnp.pad(start, ((0, 0), (0, 0), (0, padded - all_cases), (0, 0)))
    inner = 1
    while 4 * inner * inner <= blocks:
        inner *= 2
    slots = 2 * units
    dims = (local_freqs, blocks, units, cases, blocks // inner, inner)
    solution = pl.pallas_call(
        functools.partial(substitute, dims),
        out_shape=jax.ShapeDtypeStruct(start.shape, jnp.float32),
        in_specs=[pl.BlockSpec(memory_space=pltpu.SMEM), vmem, vmem, vmem],
        out_specs=vmem,
        scratch_shapes=[
            pltpu.VMEM((local_freqs, slots, 2, cases, width), jnp.float32),
            pltpu.VMEM((local_freqs, slots, 2, cases, width), jnp.float32),
            pltpu.SemaphoreType.DMA((2, local_freqs, 2)),
            pltpu.SemaphoreType.DMA((2, local_freqs, slots)),
        ],
        compiler_params=pltpu.CompilerParams(
            collective_id=0, has_side_effects=True, vmem_limit_bytes=60 * 1024 * 1024
        ),
    )(pivot_order, scaled_high, scaled_low, start)
    return solution[:, :, :all_cases]


def solution(mesh):
    placed = (
        P("freq", None, "rows"),
        P("freq", None, "rows", None),
        P("freq", None, "rows", None),
        P(),
    )
    return jax.shard_map(
        body, mesh=mesh, in_specs=placed, out_specs=P("freq", None, None, "rows"), check_vma=False
    )
```

```python
import functools

import jax
import jax.numpy as jnp
from jax import lax
from jax.experimental import pallas as pl
from jax.experimental.pallas import tpu as pltpu
from jax.sharding import PartitionSpec as P

FREQS = 16
STEPS = 256
MESH = pl.DeviceIdType.MESH


def tables(count, length):
    freq_range = jnp.arange(count, dtype=jnp.float32)
    step_range = jnp.arange(length, dtype=jnp.float32)
    angles = 2.0 * jnp.pi * (freq_range[:, None] * step_range[None, :] % length) / length
    damping = jnp.exp(step_range * (jnp.log(0.1) / length))
    return (jnp.cos(angles) * damping[None, :], -jnp.sin(angles) * damping[None, :])


def zigzag(major, minor, extent):
    return minor + lax.rem(major, 2) * (extent - 1 - 2 * minor)


def chain_position(kind, index, outer, inner):
    z, y = lax.div(index, inner), lax.rem(index, inner)
    if kind == 1:
        y = inner - 1 - y
    if kind == 3:
        z = outer - 1 - z
    if kind < 2:
        return z * inner + zigzag(z, y, inner)
    return y * outer + zigzag(y, z, outer)


def chain_index(kind, position, outer, inner):
    if kind < 2:
        z = lax.div(position, inner)
        y = zigzag(z, lax.rem(position, inner), inner)
    else:
        y = lax.div(position, outer)
        z = zigzag(y, lax.rem(position, outer), outer)
    if kind == 1:
        y = inner - 1 - y
    if kind == 3:
        z = outer - 1 - z
    return z * inner + y


def split(value):
    high = value.astype(jnp.bfloat16)
    return high, (value - high.astype(jnp.float32)).astype(jnp.bfloat16)


def triple(value, right_high, right_low):
    high, low = split(value)
    count = value.shape[0]
    both = jnp.dot(
        jnp.concatenate([high, low], axis=0), right_high, preferred_element_type=jnp.float32
    )
    rest = jnp.dot(high, right_low, preferred_element_type=jnp.float32)
    return both[:count] + both[count:] + rest


def substitute(dims, pivot_ref, high_ref, low_ref, start_ref, out_ref, right_buf, left_buf,
               send_sem, recv_sem):
    freqs, blocks, units, cases, outer, inner = dims
    width = out_ref.shape[3]
    me = lax.axis_index("rows")
    slots = right_buf.shape[1]
    last = blocks - 1
    pieces = last * units

    barrier = pltpu.get_barrier_semaphore()
    for shift in range(1, blocks):
        pl.semaphore_signal(
            barrier, inc=1, device_id={"rows": lax.rem(me + shift, blocks)}, device_id_type=MESH
        )
    out_ref[...] = start_ref[...]
    pl.semaphore_wait(barrier, last)

    my_turn = jnp.int32(0)
    for turn in range(blocks):
        my_turn = my_turn + jnp.where(pivot_ref[turn] == me, turn, 0)

    def copy(direction, f, piece, target):
        buf = (right_buf, left_buf)[direction]
        slot = lax.rem(piece, slots)
        return pltpu.make_async_remote_copy(
            src_ref=buf.at[f, slot],
            dst_ref=buf.at[f, slot],
            send_sem=send_sem.at[direction, f, lax.rem(piece, 2)],
            recv_sem=recv_sem.at[direction, f, slot],
            device_id={"rows": target},
            device_id_type=MESH,
        )

    chains = []
    for f in range(freqs):
        kind = f % 4
        position = chain_position(kind, me, outer, inner)
        right = chain_index(kind, lax.rem(position + 1, blocks), outer, inner)
        left = chain_index(kind, lax.rem(position + last, blocks), outer, inner)
        chains.append((kind, position, right, left))

    def rows_of(piece):
        return pl.ds(pl.multiple_of(lax.rem(piece, units) * cases, 8), cases)

    def flow(direction, f, piece, target, is_first, is_last):
        buf = (right_buf, left_buf)[direction]
        slot = lax.rem(piece, slots)

        @pl.when((piece >= 0) & (piece < pieces))
        def _():
            @pl.when(jnp.logical_not(is_first))
            def _():
                copy(direction, f, piece, target).wait_recv()
                mine = pivot_ref[lax.div(piece, units)] == me
                buf[f, slot] = jnp.where(mine, out_ref[f, :, rows_of(piece), :], buf[f, slot])

            @pl.when(is_first)
            def _():
                buf[f, slot] = out_ref[f, :, rows_of(piece), :]

            @pl.when(jnp.logical_not(is_last))
            def _():
                @pl.when(piece >= 2)
                def _():
                    copy(direction, f, piece - 2, target).wait_send()

                copy(direction, f, piece, target).start()

    def finish(f, kind, position, piece):
        @pl.when((piece >= 0) & (piece < pieces))
        def _():
            turn = lax.div(piece, units)
            slot = lax.rem(piece, slots)
            owner = chain_position(kind, pivot_ref[turn], outer, inner)
            solved = jnp.where(owner <= position, right_buf[f, slot], left_buf[f, slot])
            turn_block = pivot_ref[turn]
            total = triple(
                solved.reshape(2 * cases, width), high_ref[turn_block, f], low_ref[turn_block, f]
            )
            from_real, from_imag = total[:cases], total[cases:]
            real = from_real[:, :width] - from_imag[:, width:]
            imag = from_real[:, width:] + from_imag[:, :width]
            rows = rows_of(piece)
            open_still = turn < my_turn
            real_now, imag_now = out_ref[f, 0, rows, :], out_ref[f, 1, rows, :]
            out_ref[f, 0, rows, :] = jnp.where(open_still, real_now - real, real_now)
            out_ref[f, 1, rows, :] = jnp.where(open_still, imag_now - imag, imag_now)

    def tick(t, carry):
        for f, (kind, position, right, left) in enumerate(chains):
            at_start, at_end = position == 0, position == last
            flow(0, f, t - position, right, at_start, at_end)
            flow(1, f, t - (last - position), left, at_end, at_start)
            finish(f, kind, position, t - jnp.maximum(position, last - position))
        return carry

    lax.fori_loop(0, pieces + last, tick, 0)

    for f, (kind, position, right, left) in enumerate(chains):
        for piece in (pieces - 2, pieces - 1):
            @pl.when(position < last)
            def _():
                copy(0, f, jnp.int32(piece), right).wait_send()

            @pl.when(position > 0)
            def _():
                copy(1, f, jnp.int32(piece), left).wait_send()


def exchange(dims, spectra_ref, inverse_high, inverse_low, factor_ref, high_ref, low_ref,
             start_ref, core_buf, chip_buf, core_send, core_recv, chip_send, chip_recv):
    freqs, blocks, chips = dims
    cases, width = start_ref.shape[2], start_ref.shape[3]
    me = lax.axis_index("freq")
    chip, core = lax.div(me, 2), lax.rem(me, 2)
    step = pl.program_id(0) * blocks + pl.program_id(1)
    steps = freqs * blocks

    def core_copy(to_chip, f):
        return pltpu.make_async_remote_copy(
            src_ref=spectra_ref.at[to_chip * 2 + 1 - core, f],
            dst_ref=core_buf.at[to_chip, f],
            send_sem=core_send.at[to_chip, f],
            recv_sem=core_recv.at[to_chip, f],
            device_id={"freq": chip * 2 + 1 - core},
            device_id_type=MESH,
        )

    def chip_copy(shift, f):
        to_chip = lax.rem(chip + shift, chips)
        slot = chips - 1 - shift
        return pltpu.make_async_remote_copy(
            src_ref=core_buf.at[to_chip, f],
            dst_ref=chip_buf.at[slot, f],
            send_sem=chip_send.at[slot, f],
            recv_sem=chip_recv.at[slot, f],
            device_id={"freq": to_chip * 2 + core},
            device_id_type=MESH,
        )

    @pl.when(step == 0)
    def _():
        barrier = pltpu.get_barrier_semaphore()
        pl.semaphore_signal(
            barrier, inc=1, device_id={"freq": chip * 2 + 1 - core}, device_id_type=MESH
        )
        for shift in range(1, chips):
            pl.semaphore_signal(
                barrier, inc=1, device_id={"freq": lax.rem(chip + shift, chips) * 2 + core},
                device_id_type=MESH,
            )
        pl.semaphore_wait(barrier, chips)
        for f in range(freqs):
            for shift in range(1, chips + 1):
                core_copy(lax.rem(chip + shift, chips), f).start()

    for f in range(freqs):
        @pl.when(step == 1 + f)
        def _():
            for shift in range(1, chips):
                to_chip = lax.rem(chip + shift, chips)
                core_copy(to_chip, f).wait_recv()
                core_buf[to_chip, f] = core_buf[to_chip, f] + spectra_ref[to_chip * 2 + core, f]
                chip_copy(shift, f).start()

    taken = factor_ref[0]
    turned = jnp.concatenate([taken[0].T, taken[1].T], axis=0)
    f_now = pl.program_id(0)
    total = triple(turned, inverse_high[f_now], inverse_low[f_now])
    from_real, from_imag = total[:width], total[width:]
    real = from_real[:, :width] - from_imag[:, width:]
    imag = from_real[:, width:] + from_imag[:, :width]
    high_ref[0, 0], low_ref[0, 0] = split(jnp.concatenate([real, imag], axis=1))

    for f in range(freqs):
        @pl.when(step == steps - freqs + f)
        def _():
            core_copy(chip, f).wait_recv()
            value = spectra_ref[me, f] + core_buf[chip, f]
            for shift in range(1, chips):
                chip_copy(shift, f).wait_recv()
                value = value + chip_buf[chips - 1 - shift, f]
            solved = triple(value.reshape(2 * cases, width), inverse_high[f], inverse_low[f])
            start_ref[f, 0] = solved[:cases, :width] - solved[cases:, width:]
            start_ref[f, 1] = solved[:cases, width:] + solved[cases:, :width]
            for to_chip in range(chips):
                core_copy(to_chip, f).wait_send()
            for shift in range(1, chips):
                chip_copy(shift, f).wait_send()


def body(time_loads, factor, diag_inverse, pivot_order):
    high = lax.Precision.HIGH
    local_freqs = factor.shape[0]
    local_steps = time_loads.shape[0]
    all_cases = time_loads.shape[1]
    blocks = lax.axis_size("rows")
    owners = lax.axis_size("freq")
    width = diag_inverse.shape[3]
    cosine_table, sine_table = tables(FREQS, STEPS)
    table = jnp.stack([cosine_table, sine_table], axis=1)
    offset = lax.axis_index("freq") * local_steps
    part = lax.dynamic_slice_in_dim(table, offset, local_steps, 2)
    part = part.reshape(-1, local_steps)
    spectra = jnp.einsum("gn,ncr->gcr", part, time_loads, precision=high)
    spectra = spectra.reshape(owners, local_freqs, 2, all_cases, width)

    inverse = jnp.concatenate(
        [diag_inverse[:, 0].swapaxes(1, 2), diag_inverse[:, 1].swapaxes(1, 2)], axis=2
    )
    rounded = lax.reduce_precision(inverse, 8, 7)
    inverse_high = rounded.astype(jnp.bfloat16)
    inverse_low = (inverse - rounded).astype(jnp.bfloat16)

    chips = owners // 2
    vmem = pl.BlockSpec(memory_space=pltpu.VMEM)
    block = pl.BlockSpec((1, 1, width, 2 * width), lambda f, k: (k, f, 0, 0))
    scaled = jax.ShapeDtypeStruct((blocks, local_freqs, width, 2 * width), jnp.bfloat16)
    scaled_high, scaled_low, start = pl.pallas_call(
        functools.partial(exchange, (local_freqs, blocks, chips)),
        grid=(local_freqs, blocks),
        out_shape=(
            scaled, scaled,
            jax.ShapeDtypeStruct((local_freqs, 2, all_cases, width), jnp.float32),
        ),
        in_specs=[
            vmem, vmem, vmem,
            pl.BlockSpec((1, 2, width, width), lambda f, k: (f, 0, 0, k)),
        ],
        out_specs=(block, block, vmem),
        scratch_shapes=[
            pltpu.VMEM((chips, local_freqs, 2, all_cases, width), jnp.float32),
            pltpu.VMEM((max(chips - 1, 1), local_freqs, 2, all_cases, width), jnp.float32),
            pltpu.SemaphoreType.DMA((chips, local_freqs)),
            pltpu.SemaphoreType.DMA((chips, local_freqs)),
            pltpu.SemaphoreType.DMA((max(chips - 1, 1), local_freqs)),
            pltpu.SemaphoreType.DMA((max(chips - 1, 1), local_freqs)),
        ],
        compiler_params=pltpu.CompilerParams(
            collective_id=1, has_side_effects=True, vmem_limit_bytes=60 * 1024 * 1024,
            dimension_semantics=("arbitrary", "arbitrary"),
        ),
    )(spectra, inverse_high, inverse_low, factor)

    cases = 8
    while -(-all_cases // (cases + 8)) >= blocks:
        cases += 8
    units = -(-all_cases // cases)
    padded = cases * units
    if padded > all_cases:
        start = jnp.pad(start, ((0, 0), (0, 0), (0, padded - all_cases), (0, 0)))
    inner = 1
    while 4 * inner * inner <= blocks:
        inner *= 2
    slots = 2 * blocks
    dims = (local_freqs, blocks, units, cases, blocks // inner, inner)
    solution = pl.pallas_call(
        functools.partial(substitute, dims),
        out_shape=jax.ShapeDtypeStruct(start.shape, jnp.float32),
        in_specs=[pl.BlockSpec(memory_space=pltpu.SMEM), vmem, vmem, vmem],
        out_specs=vmem,
        scratch_shapes=[
            pltpu.VMEM((local_freqs, slots, 2, cases, width), jnp.float32),
            pltpu.VMEM((local_freqs, slots, 2, cases, width), jnp.float32),
            pltpu.SemaphoreType.DMA((2, local_freqs, 2)),
            pltpu.SemaphoreType.DMA((2, local_freqs, slots)),
        ],
        compiler_params=pltpu.CompilerParams(
            collective_id=0, has_side_effects=True, vmem_limit_bytes=60 * 1024 * 1024
        ),
    )(pivot_order, scaled_high, scaled_low, start)
    return solution[:, :, :all_cases]


def solution(mesh):
    placed = (
        P("freq", None, "rows"),
        P("freq", None, "rows", None),
        P("freq", None, "rows", None),
        P(),
    )
    return jax.shard_map(
        body, mesh=mesh, in_specs=placed, out_specs=P("freq", None, None, "rows"), check_vma=False
    )
```

```python
import functools

import jax
import jax.numpy as jnp
from jax import lax
from jax.experimental import pallas as pl
from jax.experimental.pallas import tpu as pltpu
from jax.sharding import PartitionSpec as P

FREQS = 16
STEPS = 256
MESH = pl.DeviceIdType.MESH


def tables(count, length):
    freq_range = jnp.arange(count, dtype=jnp.float32)
    step_range = jnp.arange(length, dtype=jnp.float32)
    angles = 2.0 * jnp.pi * (freq_range[:, None] * step_range[None, :] % length) / length
    damping = jnp.exp(step_range * (jnp.log(0.1) / length))
    return (jnp.cos(angles) * damping[None, :], -jnp.sin(angles) * damping[None, :])


def zigzag(major, minor, extent):
    return minor + lax.rem(major, 2) * (extent - 1 - 2 * minor)


def chain_position(kind, index, outer, inner):
    z, y = lax.div(index, inner), lax.rem(index, inner)
    if kind == 1:
        y = inner - 1 - y
    if kind == 3:
        z = outer - 1 - z
    if kind < 2:
        return z * inner + zigzag(z, y, inner)
    return y * outer + zigzag(y, z, outer)


def chain_index(kind, position, outer, inner):
    if kind < 2:
        z = lax.div(position, inner)
        y = zigzag(z, lax.rem(position, inner), inner)
    else:
        y = lax.div(position, outer)
        z = zigzag(y, lax.rem(position, outer), outer)
    if kind == 1:
        y = inner - 1 - y
    if kind == 3:
        z = outer - 1 - z
    return z * inner + y


def split(value):
    high = value.astype(jnp.bfloat16)
    return high, (value - high.astype(jnp.float32)).astype(jnp.bfloat16)


def triple(value, right_high, right_low):
    high, low = split(value)
    count = value.shape[0]
    both = jnp.dot(
        jnp.concatenate([high, low], axis=0), right_high, preferred_element_type=jnp.float32
    )
    rest = jnp.dot(high, right_low, preferred_element_type=jnp.float32)
    return both[:count] + both[count:] + rest


def substitute(dims, pivot_ref, high_ref, low_ref, start_ref, out_ref, right_buf, left_buf,
               send_sem, recv_sem):
    freqs, blocks, units, cases, outer, inner = dims
    width = out_ref.shape[3]
    me = lax.axis_index("rows")
    slots = right_buf.shape[1]
    last = blocks - 1
    pieces = last * units

    barrier = pltpu.get_barrier_semaphore()
    for shift in range(1, blocks):
        pl.semaphore_signal(
            barrier, inc=1, device_id={"rows": lax.rem(me + shift, blocks)}, device_id_type=MESH
        )
    out_ref[...] = start_ref[...]
    pl.semaphore_wait(barrier, last)

    my_turn = jnp.int32(0)
    for turn in range(blocks):
        my_turn = my_turn + jnp.where(pivot_ref[turn] == me, turn, 0)

    def copy(direction, f, piece, target):
        buf = (right_buf, left_buf)[direction]
        slot = lax.rem(piece, slots)
        return pltpu.make_async_remote_copy(
            src_ref=buf.at[f, slot],
            dst_ref=buf.at[f, slot],
            send_sem=send_sem.at[direction, f, lax.rem(piece, 2)],
            recv_sem=recv_sem.at[direction, f, slot],
            device_id={"rows": target},
            device_id_type=MESH,
        )

    chains = []
    for f in range(freqs):
        kind = f % 4
        position = chain_position(kind, me, outer, inner)
        right = chain_index(kind, lax.rem(position + 1, blocks), outer, inner)
        left = chain_index(kind, lax.rem(position + last, blocks), outer, inner)
        chains.append((kind, position, right, left))

    def rows_of(piece):
        return pl.ds(pl.multiple_of(lax.rem(piece, units) * cases, 8), cases)

    def flow(direction, f, piece, target, is_first, is_last):
        buf = (right_buf, left_buf)[direction]
        slot = lax.rem(piece, slots)

        @pl.when((piece >= 0) & (piece < pieces))
        def _():
            @pl.when(jnp.logical_not(is_first))
            def _():
                copy(direction, f, piece, target).wait_recv()
                mine = pivot_ref[lax.div(piece, units)] == me
                buf[f, slot] = jnp.where(mine, out_ref[f, :, rows_of(piece), :], buf[f, slot])

            @pl.when(is_first)
            def _():
                buf[f, slot] = out_ref[f, :, rows_of(piece), :]

            @pl.when(jnp.logical_not(is_last))
            def _():
                @pl.when(piece >= 2)
                def _():
                    copy(direction, f, piece - 2, target).wait_send()

                copy(direction, f, piece, target).start()

    def finish(f, kind, position, piece):
        @pl.when((piece >= 0) & (piece < pieces))
        def _():
            turn = lax.div(piece, units)
            slot = lax.rem(piece, slots)
            owner = chain_position(kind, pivot_ref[turn], outer, inner)
            solved = jnp.where(owner <= position, right_buf[f, slot], left_buf[f, slot])
            turn_block = pivot_ref[turn]
            total = triple(
                solved.reshape(2 * cases, width), high_ref[turn_block, f], low_ref[turn_block, f]
            )
            from_real, from_imag = total[:cases], total[cases:]
            real = from_real[:, :width] - from_imag[:, width:]
            imag = from_real[:, width:] + from_imag[:, :width]
            rows = rows_of(piece)
            open_still = turn < my_turn
            real_now, imag_now = out_ref[f, 0, rows, :], out_ref[f, 1, rows, :]
            out_ref[f, 0, rows, :] = jnp.where(open_still, real_now - real, real_now)
            out_ref[f, 1, rows, :] = jnp.where(open_still, imag_now - imag, imag_now)

    def tick(t, carry):
        for f, (kind, position, right, left) in enumerate(chains):
            at_start, at_end = position == 0, position == last
            flow(0, f, t - position, right, at_start, at_end)
            flow(1, f, t - (last - position), left, at_end, at_start)
            finish(f, kind, position, t - jnp.maximum(position, last - position))
        return carry

    lax.fori_loop(0, pieces + last, tick, 0)

    for f, (kind, position, right, left) in enumerate(chains):
        for piece in (pieces - 2, pieces - 1):
            @pl.when(position < last)
            def _():
                copy(0, f, jnp.int32(piece), right).wait_send()

            @pl.when(position > 0)
            def _():
                copy(1, f, jnp.int32(piece), left).wait_send()


def exchange(dims, spectra_ref, inverse_ref, factor_ref, high_ref, low_ref, start_ref,
             inverse_high, inverse_low, core_buf, chip_buf, core_send, core_recv, chip_send,
             chip_recv):
    freqs, blocks, chips = dims
    cases, width = start_ref.shape[2], start_ref.shape[3]
    me = lax.axis_index("freq")
    chip, core = lax.div(me, 2), lax.rem(me, 2)
    step = pl.program_id(0) * blocks + pl.program_id(1)
    steps = freqs * blocks

    def core_copy(to_chip, f):
        return pltpu.make_async_remote_copy(
            src_ref=spectra_ref.at[to_chip * 2 + 1 - core, f],
            dst_ref=core_buf.at[to_chip, f],
            send_sem=core_send.at[to_chip, f],
            recv_sem=core_recv.at[to_chip, f],
            device_id={"freq": chip * 2 + 1 - core},
            device_id_type=MESH,
        )

    def chip_copy(shift, f):
        to_chip = lax.rem(chip + shift, chips)
        slot = chips - 1 - shift
        return pltpu.make_async_remote_copy(
            src_ref=core_buf.at[to_chip, f],
            dst_ref=chip_buf.at[slot, f],
            send_sem=chip_send.at[slot, f],
            recv_sem=chip_recv.at[slot, f],
            device_id={"freq": to_chip * 2 + core},
            device_id_type=MESH,
        )

    @pl.when(step == 0)
    def _():
        barrier = pltpu.get_barrier_semaphore()
        pl.semaphore_signal(
            barrier, inc=1, device_id={"freq": chip * 2 + 1 - core}, device_id_type=MESH
        )
        for shift in range(1, chips):
            pl.semaphore_signal(
                barrier, inc=1, device_id={"freq": lax.rem(chip + shift, chips) * 2 + core},
                device_id_type=MESH,
            )
        pl.semaphore_wait(barrier, chips)
        for f in range(freqs):
            for shift in range(1, chips):
                core_copy(lax.rem(chip + shift, chips), f).start()
        for f in range(freqs):
            core_copy(chip, f).start()
        for f in range(freqs):
            inverse_high[f], inverse_low[f] = split(
                jnp.concatenate([inverse_ref[f, 0].T, inverse_ref[f, 1].T], axis=1)
            )

    for f in range(freqs):
        @pl.when(step == 1 + f)
        def _():
            for shift in range(1, chips):
                to_chip = lax.rem(chip + shift, chips)
                core_copy(to_chip, f).wait_recv()
                core_buf[to_chip, f] = core_buf[to_chip, f] + spectra_ref[to_chip * 2 + core, f]
                chip_copy(shift, f).start()

    taken = factor_ref[0]
    turned = jnp.concatenate([taken[0].T, taken[1].T], axis=0)
    f_now = pl.program_id(0)
    total = triple(turned, inverse_high[f_now], inverse_low[f_now])
    from_real, from_imag = total[:width], total[width:]
    real = from_real[:, :width] - from_imag[:, width:]
    imag = from_real[:, width:] + from_imag[:, :width]
    high_ref[0, 0], low_ref[0, 0] = split(jnp.concatenate([real, imag], axis=1))

    for f in range(freqs):
        @pl.when(step == steps - freqs + f)
        def _():
            core_copy(chip, f).wait_recv()
            value = spectra_ref[me, f] + core_buf[chip, f]
            for shift in range(1, chips):
                chip_copy(shift, f).wait_recv()
                value = value + chip_buf[chips - 1 - shift, f]
            solved = triple(value.reshape(2 * cases, width), inverse_high[f], inverse_low[f])
            start_ref[f, 0] = solved[:cases, :width] - solved[cases:, width:]
            start_ref[f, 1] = solved[:cases, width:] + solved[cases:, :width]
            for to_chip in range(chips):
                core_copy(to_chip, f).wait_send()
            for shift in range(1, chips):
                chip_copy(shift, f).wait_send()


def body(time_loads, factor, diag_inverse, pivot_order):
    high = lax.Precision.HIGH
    local_freqs = factor.shape[0]
    local_steps = time_loads.shape[0]
    all_cases = time_loads.shape[1]
    blocks = lax.axis_size("rows")
    owners = lax.axis_size("freq")
    width = diag_inverse.shape[3]
    cosine_table, sine_table = tables(FREQS, STEPS)
    table = jnp.stack([cosine_table, sine_table], axis=1)
    offset = lax.axis_index("freq") * local_steps
    part = lax.dynamic_slice_in_dim(table, offset, local_steps, 2)
    part = part.reshape(-1, local_steps)
    spectra = jnp.einsum("gn,ncr->gcr", part, time_loads, precision=high)
    spectra = spectra.reshape(owners, local_freqs, 2, all_cases, width)

    chips = owners // 2
    vmem = pl.BlockSpec(memory_space=pltpu.VMEM)
    block = pl.BlockSpec((1, 1, width, 2 * width), lambda f, k: (k, f, 0, 0))
    scaled = jax.ShapeDtypeStruct((blocks, local_freqs, width, 2 * width), jnp.bfloat16)
    scaled_high, scaled_low, start = pl.pallas_call(
        functools.partial(exchange, (local_freqs, blocks, chips)),
        grid=(local_freqs, blocks),
        out_shape=(
            scaled, scaled,
            jax.ShapeDtypeStruct((local_freqs, 2, all_cases, width), jnp.float32),
        ),
        in_specs=[
            vmem, vmem,
            pl.BlockSpec((1, 2, width, width), lambda f, k: (f, 0, 0, k)),
        ],
        out_specs=(block, block, vmem),
        scratch_shapes=[
            pltpu.VMEM((local_freqs, width, 2 * width), jnp.bfloat16),
            pltpu.VMEM((local_freqs, width, 2 * width), jnp.bfloat16),
            pltpu.VMEM((chips, local_freqs, 2, all_cases, width), jnp.float32),
            pltpu.VMEM((max(chips - 1, 1), local_freqs, 2, all_cases, width), jnp.float32),
            pltpu.SemaphoreType.DMA((chips, local_freqs)),
            pltpu.SemaphoreType.DMA((chips, local_freqs)),
            pltpu.SemaphoreType.DMA((max(chips - 1, 1), local_freqs)),
            pltpu.SemaphoreType.DMA((max(chips - 1, 1), local_freqs)),
        ],
        compiler_params=pltpu.CompilerParams(
            collective_id=1, has_side_effects=True, vmem_limit_bytes=60 * 1024 * 1024,
            dimension_semantics=("arbitrary", "arbitrary"),
        ),
    )(spectra, diag_inverse, factor)

    cases = 8
    while -(-all_cases // (cases + 8)) >= blocks:
        cases += 8
    units = -(-all_cases // cases)
    padded = cases * units
    if padded > all_cases:
        start = jnp.pad(start, ((0, 0), (0, 0), (0, padded - all_cases), (0, 0)))
    inner = 1
    while 4 * inner * inner <= blocks:
        inner *= 2
    slots = 2 * blocks
    dims = (local_freqs, blocks, units, cases, blocks // inner, inner)
    solution = pl.pallas_call(
        functools.partial(substitute, dims),
        out_shape=jax.ShapeDtypeStruct(start.shape, jnp.float32),
        in_specs=[pl.BlockSpec(memory_space=pltpu.SMEM), vmem, vmem, vmem],
        out_specs=vmem,
        scratch_shapes=[
            pltpu.VMEM((local_freqs, slots, 2, cases, width), jnp.float32),
            pltpu.VMEM((local_freqs, slots, 2, cases, width), jnp.float32),
            pltpu.SemaphoreType.DMA((2, local_freqs, 2)),
            pltpu.SemaphoreType.DMA((2, local_freqs, slots)),
        ],
        compiler_params=pltpu.CompilerParams(
            collective_id=0, has_side_effects=True, vmem_limit_bytes=60 * 1024 * 1024
        ),
    )(pivot_order, scaled_high, scaled_low, start)
    return solution[:, :, :all_cases]


def solution(mesh):
    placed = (
        P("freq", None, "rows"),
        P("freq", None, "rows", None),
        P("freq", None, "rows", None),
        P(),
    )
    return jax.shard_map(
        body, mesh=mesh, in_specs=placed, out_specs=P("freq", None, None, "rows"), check_vma=False
    )
```
